32 devices in a mesh: ctx: 8 (over z, y), tp: 4 (over x, core).
Axes of the slice: x: 2, y: 2, z: 4, core: 2. Of those that a mesh axis runs over, the one named last changes fastest.
Arguments:
- queries: bfloat16 [4096, 8192], P('ctx', 'tp'), may hold values from -6 to 6
- keys: bfloat16 [4096, 1024], P('ctx', 'tp'), may hold values from -6 to 6
- values: bfloat16 [4096, 1024], P('ctx', 'tp'), may hold values from -6 to 6
- block_plan: int32 [8, 4], replicated, may hold values from 0 to 7, as said below
- doc_lengths: int32 [16], replicated, may hold values from 1 to 2048, 4096 in all
- scan_input: bfloat16 [4096, 16384], P('ctx', 'tp'), may hold values from -6 to 6
- gate_input: bfloat16 [4096, 16384], P('ctx', 'tp'), may hold values from -600 to 600
- step_size: bfloat16 [4096, 256], P('ctx', 'tp'), may hold values from 0 to 6
- decay_rate: float32 [256], P('tp'), may hold values from 0.05 to 1.5
- state_in: bfloat16 [4096, 16], P('ctx'), may hold values from -6 to 6
- state_out: bfloat16 [4096, 16], P('ctx'), may hold values from -6 to 6
- skip_gain: float32 [256], P('tp'), may hold values from 0.5 to 1.5
- norm_gain: float32 [16384], P('tp'), may hold values from 0.5 to 1.5
Outputs:
- attn_out: bfloat16 [4096, 8192], P('ctx', 'tp')
- mamba_out: bfloat16 [4096, 16384], P('ctx', 'tp')
The draws below stay inside these ranges and needn't reach their ends.
Inputs may be any that keep to these rules, and one draw needn't show every extreme that they name: `block_plan`: each row lists 4 distinct offsets, the first of them 0.
All inputs are finite; a program needn't handle non-finite values.
Results may differ from the reference program's by a relative error of at most 0.007.
Values may be sent and summed in bfloat16 or wider, within the bound.
A program may use at most 128 MiB of HBM per device.

```python
import math
import jax
import jax.numpy as jnp
import numpy as np
from jax import lax

QUERY_HEADS = 64
KEY_VALUE_HEADS = 8
HEAD_WIDTH = 128
INNER = 16384
STATE_WIDTH = 16
DECAY_CHANNELS = 64
SPAN = 8
PICKED_BLOCKS = 4
BLOCK_TOKENS = 512
TOKEN_TOTAL = 4096
BLOCK_TOTAL = 8
NDOC = 16
DOCMAX = 2048
SCAN_HEAD_COUNT = 256


def log_uniform(key, shape, low, high):
    return jnp.exp(jax.random.uniform(key, shape, jnp.float32, jnp.log(low), jnp.log(high)))


def draw_queries(key, part):
    start_point = jnp.clip(jax.random.normal(jax.random.fold_in(key, 11), (TOKEN_TOTAL, QUERY_HEADS * HEAD_WIDTH), jnp.float32), -6.0, 6.0)
    return start_point.astype(jnp.bfloat16)


def draw_keys(key, part):
    start_point = jnp.clip(jax.random.normal(jax.random.fold_in(key, 12), (TOKEN_TOTAL, KEY_VALUE_HEADS * HEAD_WIDTH), jnp.float32), -6.0, 6.0)
    return start_point.astype(jnp.bfloat16)


def draw_block_plan(key, part):
    scores = jax.random.randint(jax.random.fold_in(key, 13), (BLOCK_TOTAL, SPAN - 1), 0, 1 << 20) * SPAN
    scores = scores + jnp.arange(SPAN - 1, dtype=jnp.int32)[None, :]
    scores = scores.at[0, SPAN - 2].set(-1)
    ranking = jnp.argsort(scores, axis=1)
    picked = (ranking[:, :PICKED_BLOCKS - 1] + 1).astype(jnp.int32)
    return jnp.concatenate([jnp.zeros((BLOCK_TOTAL, 1), jnp.int32), picked], axis=1)


def head_law(key):
    share = 0.5
    slow_heads = jax.random.uniform(jax.random.fold_in(key, 5301), (SCAN_HEAD_COUNT,), jnp.float32) < share
    rate = jnp.where(slow_heads, log_uniform(jax.random.fold_in(key, 5302), (SCAN_HEAD_COUNT,), 0.05, 0.09), log_uniform(jax.random.fold_in(key, 5303), (SCAN_HEAD_COUNT,), 0.5, 1.5))
    step_start_value = jnp.where(slow_heads, log_uniform(jax.random.fold_in(key, 5304), (SCAN_HEAD_COUNT,), 0.002, 0.004), log_uniform(jax.random.fold_in(key, 5305), (SCAN_HEAD_COUNT,), 0.02, 0.05))
    return (rate, step_start_value)


def draw_decay_rate(key, part):
    rate, step_start_value = head_law(key)
    return rate.astype(jnp.float32)


def draw_step_size(key, part):
    rate, step_start_value = head_law(key)
    coarse_scores = log_uniform(jax.random.fold_in(key, 5306), (TOKEN_TOTAL, SCAN_HEAD_COUNT), 0.5, 2.0)
    token_runs = jax.random.randint(jax.random.fold_in(key, 5307), (TOKEN_TOTAL,), 0, 4 * BLOCK_TOKENS) == 0
    value_result = step_start_value[None, :] * coarse_scores + 5.0 * token_runs.astype(jnp.float32)[:, None]
    return value_result.astype(jnp.bfloat16)


def draw_gate_input(key, part):
    channel_scale = 10.0 ** (jnp.arange(INNER, dtype=jnp.float32) / INNER)
    channel_scale = channel_scale * log_uniform(jax.random.fold_in(key, 21), (INNER,), 0.7, 1.4)
    row_scale = log_uniform(jax.random.fold_in(key, 22), (TOKEN_TOTAL, 1), 1.0, 10.0)
    start_point = jnp.clip(jax.random.normal(jax.random.fold_in(key, 24), (TOKEN_TOTAL, INNER), jnp.float32), -4.0, 4.0)
    return (start_point * channel_scale[None, :] * row_scale).astype(jnp.bfloat16)


def level_of(own_key, shape, pieces, smallest, high):
    level, own = 1.0, jax.random.fold_in(own_key, 6)
    for axis_at, blocks in pieces:
        steps = jnp.exp(jax.random.uniform(jax.random.fold_in(own, axis_at), (blocks,), jnp.float32, smallest / len(pieces), high / len(pieces)))
        level = level * jnp.repeat(steps, shape[axis_at] // blocks).reshape([-1 if axis == axis_at else 1 for axis in range(len(shape))])
    return level


def split_up(amount, total, limit, skew):
    loads = [(1 << 20) // math.isqrt(standing ** skew) + 1 for standing in range(2, amount + 1)]
    rest, given = total - limit - (amount - 1), [1] * (amount - 1)
    while rest > 0:
        movable = [i for i in range(amount - 1) if given[i] < limit]
        mass, budget = sum([loads[i] for i in movable]), rest
        for i in movable:
            more = min(limit - given[i], max(1, budget * loads[i] // mass), rest)
            given[i] = given[i] + more
            rest = rest - more
    return np.array([limit] + given)


def uneven(rng, number_of, total, bound, lean):
    if number_of == 2:
        one = jax.random.randint(rng, (), max(1, total - bound), min(bound, total - 1) + 1)
        return jnp.stack([one, total - one])
    sizes = jnp.asarray(split_up(number_of, total, bound, lean), jnp.int32)
    couples = (number_of - 1) // 2
    donor, taker = sizes[1:1 + 2 * couples:2], sizes[2:2 + 2 * couples:2]
    room = jnp.minimum(donor - 1, bound - taker)
    shifted = jax.random.randint(jax.random.fold_in(rng, 1), (couples,), 0, 1 << 20) % (room + 1)
    sizes = sizes.at[1:1 + 2 * couples:2].set(donor - shifted).at[2:2 + 2 * couples:2].set(taker + shifted)
    return sizes[jax.random.permutation(jax.random.fold_in(rng, 2), number_of)]


def scatter_about(rng, shape, deviation, limit, pieces=(), kind=jnp.bfloat16):
    drawn = jax.random.normal(rng, shape, jnp.float32) * deviation
    if len(pieces) > 0:
        drawn = level_of(rng, shape, pieces, -0.22, 0.18) * drawn
    return jnp.clip(drawn, min=-limit, max=limit).astype(kind)


def setup_inputs(seed: int = 0) -> dict:
    splits = jax.random.split(jax.random.key(seed), 14)
    queries = draw_queries(jax.random.fold_in(splits[13], 71), 0)
    keys = draw_keys(jax.random.fold_in(splits[13], 71), 0)
    values = scatter_about(splits[2], (TOKEN_TOTAL, KEY_VALUE_HEADS * HEAD_WIDTH), 1.0, 6.0, ((0, 8), (1, 4)))
    block_plan = draw_block_plan(jax.random.fold_in(splits[13], 71), 0)
    doc_lengths = uneven(splits[4], NDOC, TOKEN_TOTAL, DOCMAX, 2).astype(jnp.int32)
    scan_input = scatter_about(splits[5], (TOKEN_TOTAL, INNER), 1.0, 6.0, ((0, 8), (1, 4)))
    gate_input = draw_gate_input(jax.random.fold_in(splits[13], 71), 0)
    step_size = draw_step_size(jax.random.fold_in(splits[13], 71), 0)
    decay_rate = draw_decay_rate(jax.random.fold_in(splits[13], 71), 0)
    state_in = scatter_about(splits[9], (TOKEN_TOTAL, STATE_WIDTH), 1.0, 6.0, ((0, 8),))
    state_out = scatter_about(splits[10], (TOKEN_TOTAL, STATE_WIDTH), 1.0, 6.0, ((0, 8),))
    skip_gain = jnp.clip(0.5 + 1.0 * jax.random.uniform(splits[11], (SCAN_HEAD_COUNT,), jnp.float32) ** level_of(splits[11], (SCAN_HEAD_COUNT,), ((0, 4),), -0.2, 0.2), 0.5, 1.5)
    norm_gain = jnp.clip(1.0 + 0.1 * jax.random.normal(splits[12], (INNER,), jnp.float32), 0.5, 1.5)
    return dict(queries=queries, keys=keys, values=values, block_plan=block_plan, doc_lengths=doc_lengths, scan_input=scan_input, gate_input=gate_input, step_size=step_size, decay_rate=decay_rate, state_in=state_in, state_out=state_out, skip_gain=skip_gain, norm_gain=norm_gain)


def doc_index(positions, doc_lengths):
    doc_ends = jnp.cumsum(doc_lengths).astype(jnp.int32)
    return lax.optimization_barrier(jnp.sum((positions[:, None] >= doc_ends[None, :]).astype(jnp.int32), axis=1)).astype(jnp.int32)

def attention(queries, keys, values, block_plan, doc_lengths):
    query_group_width = QUERY_HEADS // KEY_VALUE_HEADS
    scale_factor = HEAD_WIDTH ** (-0.5)
    every_query = queries.reshape(BLOCK_TOTAL, BLOCK_TOKENS, KEY_VALUE_HEADS, query_group_width, HEAD_WIDTH)
    every_key = keys.reshape(BLOCK_TOTAL, BLOCK_TOKENS, KEY_VALUE_HEADS, HEAD_WIDTH)
    every_value = values.reshape(BLOCK_TOTAL, BLOCK_TOKENS, KEY_VALUE_HEADS, HEAD_WIDTH)
    offsets_row = jnp.arange(BLOCK_TOKENS, dtype=jnp.int32)

    def one_block(block_index):
        query_block = lax.dynamic_index_in_dim(every_query, block_index, 0, keepdims=False)
        chosen = block_index - block_plan[block_index]
        valid = chosen >= 0
        clamped_block = jnp.maximum(chosen, 0).astype(jnp.int32)
        picked_keys = every_key[clamped_block].reshape(PICKED_BLOCKS * BLOCK_TOKENS, KEY_VALUE_HEADS, HEAD_WIDTH)
        picked_values = every_value[clamped_block].reshape(PICKED_BLOCKS * BLOCK_TOKENS, KEY_VALUE_HEADS, HEAD_WIDTH)
        query_position = block_index * BLOCK_TOKENS + offsets_row
        key_position = (clamped_block[:, None] * BLOCK_TOKENS + offsets_row[None, :]).reshape(-1)
        key_valid = jnp.repeat(valid, BLOCK_TOKENS)
        allowed = key_valid[None, :] & (key_position[None, :] <= query_position[:, None])
        allowed = allowed & (doc_index(key_position, doc_lengths)[None, :] == doc_index(query_position, doc_lengths)[:, None])
        scores = jnp.einsum('tkgd,skd->kgts', query_block.astype(jnp.float32), picked_keys.astype(jnp.float32)) * scale_factor
        masked = jnp.where(allowed[None, None], scores, -1e+30)
        row_peak = lax.optimization_barrier(jnp.max(masked, axis=-1, keepdims=True))
        weights = jnp.where(allowed[None, None], jnp.exp(masked - row_peak), 0.0)
        denominator = lax.optimization_barrier(jnp.sum(weights, axis=-1))
        rounded = lax.optimization_barrier(weights.astype(jnp.bfloat16)).astype(jnp.float32)
        weighted = jnp.einsum('kgts,skd->tkgd', rounded, picked_values.astype(jnp.float32))
        result = weighted / jnp.transpose(denominator, (2, 0, 1))[..., None]
        return result.astype(jnp.bfloat16).reshape(BLOCK_TOKENS, QUERY_HEADS * HEAD_WIDTH)
    blocks_out = lax.map(one_block, jnp.arange(BLOCK_TOTAL, dtype=jnp.int32))
    return blocks_out.reshape(TOKEN_TOTAL, QUERY_HEADS * HEAD_WIDTH)

def selective_scan(scan_input, gate_input, step_size, decay_rate, state_in, state_out, skip_gain, norm_gain, doc_lengths):
    positions = jnp.arange(TOKEN_TOTAL, dtype=jnp.int32)
    token_doc = doc_index(positions, doc_lengths)
    first_flag = jnp.concatenate([jnp.ones((1,), dtype=bool), token_doc[1:] != token_doc[:-1]])

    def one_token(hidden_state, inputs):
        input_token, gate_token, step_token, in_token, out_token, first_token = inputs
        input_single = input_token.astype(jnp.float32).reshape(SCAN_HEAD_COUNT, DECAY_CHANNELS)
        step_float = step_token.astype(jnp.float32)
        decay = jnp.where(first_token, jnp.float32(0.0), jnp.exp(-decay_rate * step_float))
        drive_value = lax.optimization_barrier((step_float[:, None] * input_single).astype(jnp.bfloat16)).astype(jnp.float32)
        drive = drive_value[:, :, None] * in_token.astype(jnp.float32)[None, None, :]
        hidden_state = decay[:, None, None] * hidden_state + drive
        scan_y = lax.optimization_barrier(jnp.sum(hidden_state * out_token.astype(jnp.float32)[None, None, :], axis=-1)) + skip_gain[:, None] * input_single
        gated = scan_y.reshape(INNER) * jax.nn.silu(gate_token.astype(jnp.float32))
        result = gated * lax.rsqrt(jnp.mean(gated * gated) + 1e-05) * norm_gain
        return (hidden_state, result.astype(jnp.bfloat16))
    starting_state = jnp.zeros((SCAN_HEAD_COUNT, DECAY_CHANNELS, STATE_WIDTH), jnp.float32)
    _, mamba_out = lax.scan(one_token, starting_state, (scan_input, gate_input, step_size, state_in, state_out, first_flag))
    return mamba_out

def reference(queries, keys, values, block_plan, doc_lengths, scan_input, gate_input, step_size, decay_rate, state_in, state_out, skip_gain, norm_gain):
    attn_out = attention(queries, keys, values, block_plan, doc_lengths)
    mamba_out = selective_scan(scan_input, gate_input, step_size, decay_rate, state_in, state_out, skip_gain, norm_gain, doc_lengths)
    return (attn_out, mamba_out)
```

```python
import functools
import math

import jax
import jax.numpy as jnp
from jax import lax
from jax.experimental import pallas as pl
from jax.experimental.pallas import tpu as pltpu
from jax.sharding import PartitionSpec as P


HEAD_WIDTH = 128
SPAN = 8
GROUP = 8
LANES = 128
NEG = -1e30
VMEM_LIMIT = None


def longest_reach(ctx):
    return min(ctx - 1, 4 if ctx <= SPAN else SPAN)


def fold_head(width, keys, value_t, queries, bias, before):
    scale = width**-0.5 * math.log2(math.e)
    scores = lax.dot_general(
        keys, queries, (((1,), (1,)), ((), ())), preferred_element_type=jnp.float32
    )
    scores = scores * scale + bias
    top = jnp.max(scores, axis=0, keepdims=True)
    if before is not None:
        top = jnp.maximum(top, before[0])
    weights = jnp.exp2(scores - top)
    part = jnp.sum(weights, axis=0, keepdims=True)
    weighted = jnp.dot(value_t, weights.astype(jnp.bfloat16), preferred_element_type=jnp.float32)
    if before is not None:
        factor = jnp.exp2(before[0] - top)
        part = part + before[1] * factor
        weighted = weighted + before[2] * factor
    return top, part, weighted


def attention_kernel(width, pieces, active, distances, start, q, peak_in, total_in, acc_in, *refs):
    keys, values = refs[: 2 * pieces : 2], refs[1 : 2 * pieces : 2]
    out, bias, peak, total, acc = refs[2 * pieces :]
    rows = q.shape[0]
    heads = q.shape[1] // width
    key_at = lax.broadcasted_iota(jnp.int32, (rows, rows), 0)
    peak[...] = peak_in[...]
    total[...] = total_in[...]
    acc[...] = acc_in[...].astype(jnp.float32) * total_in[...]

    def fold(piece):
        bias[...] = jnp.where(key_at - distances[piece] * rows >= start[...], 0.0, NEG)
        value_t = values[piece][...].T

        def one_head(h, _):
            at = pl.ds(pl.multiple_of(h * width, width), width)
            peak[h], total[h], acc[h] = fold_head(
                width,
                keys[piece][...],
                value_t,
                q[:, at],
                bias[...],
                (peak[h], total[h], acc[h]),
            )
            return 0

        lax.fori_loop(0, heads, one_head, 0, unroll=2)

    for piece in range(pieces):
        pl.when(active[piece] > 0)(functools.partial(fold, piece))

    def finish(h, _):
        at = pl.ds(pl.multiple_of(h * width, width), width)
        out[:, at] = (acc[h] / total[h]).T.astype(out.dtype)
        return 0

    lax.fori_loop(0, heads, finish, 0)


def attention_sums(rows, heads, kv_heads):
    shapes = [(heads, 1, rows), (heads, 1, rows), (heads, HEAD_WIDTH, rows)]
    specs = [pl.BlockSpec((heads // kv_heads,) + s[1:], lambda i, *a: (i, 0, 0)) for s in shapes]
    kinds = [jnp.float32, jnp.float32, jnp.bfloat16]
    return [jax.ShapeDtypeStruct(s, k) for s, k in zip(shapes, kinds)], specs


def attend_cost(q, blocks):
    return pl.CostEstimate(
        flops=4 * blocks * q.shape[0] * q.size,
        bytes_accessed=8 * q.size,
        transcendentals=blocks * q.shape[0] * q.size // HEAD_WIDTH,
    )


def attention(q, sums, blocks, start, active, distances, kv_heads):
    rows = q.shape[0]
    wide = q.shape[1] // kv_heads
    pieces = len(blocks)
    heads = wide // HEAD_WIDTH
    specs = [
        pl.BlockSpec((1, rows), lambda i, a, d: (0, 0)),
        pl.BlockSpec((rows, wide), lambda i, a, d: (0, i)),
    ] + attention_sums(rows, q.shape[1] // HEAD_WIDTH, kv_heads)[1]
    operands = [start, q, *sums]
    for block, slot in blocks:
        for first in (0, kv_heads):
            specs.append(
                pl.BlockSpec(
                    (None, rows, HEAD_WIDTH), lambda i, a, d, s=slot, f=first: (s, 0, f + i)
                )
            )
            operands.append(block)
    return pl.pallas_call(
        functools.partial(attention_kernel, HEAD_WIDTH, pieces),
        out_shape=jax.ShapeDtypeStruct(q.shape, jnp.bfloat16),
        grid_spec=pltpu.PrefetchScalarGridSpec(
            num_scalar_prefetch=2,
            grid=(kv_heads,),
            in_specs=specs,
            out_specs=pl.BlockSpec((rows, wide), lambda i, a, d: (0, i)),
            scratch_shapes=[
                pltpu.VMEM((rows, rows), jnp.float32),
                pltpu.VMEM((heads, 1, rows), jnp.float32),
                pltpu.VMEM((heads, 1, rows), jnp.float32),
                pltpu.VMEM((heads, HEAD_WIDTH, rows), jnp.float32),
            ],
        ),
        cost_estimate=attend_cost(q, 3),
        name="attend",
    )(active, distances, *operands)


def split3(v):
    high = v.astype(jnp.bfloat16)
    rest = v - high.astype(jnp.float32)
    mid = rest.astype(jnp.bfloat16)
    low = (rest - mid.astype(jnp.float32)).astype(jnp.bfloat16)
    return high, mid, low


def widen(rows, heads, first, width, lanes):
    head = lax.rem(lax.broadcasted_iota(jnp.int32, (rows, lanes), 0), heads)
    wanted = first + lax.broadcasted_iota(jnp.int32, (rows, lanes), 1) // width
    return jnp.where(head == wanted, 1.0, 0.0).astype(jnp.bfloat16)


def widen_pairs(rows, heads, first, n, lanes):
    head = lax.rem(lax.broadcasted_iota(jnp.int32, (rows, lanes), 0), heads)
    lane = lax.broadcasted_iota(jnp.int32, (rows, lanes), 1)
    wanted = first + 2 * (lane // LANES) + lax.rem(lane, 2 * n) // n
    return jnp.where(head == wanted, 1.0, 0.0).astype(jnp.bfloat16)


def split2(v):
    high = v.astype(jnp.bfloat16)
    return high, (v - high.astype(jnp.float32)).astype(jnp.bfloat16)


def left_parts(v, n):
    high, low = split2(v)
    part = lax.broadcasted_iota(jnp.int32, v.shape, 1) // (2 * n)
    return jnp.where(part == 1, low, jnp.where(part < 3, high, jnp.zeros_like(high)))


def right_parts(v):
    high, low = split2(v)
    rest = jnp.zeros((LANES - 3 * v.shape[0], v.shape[1]), jnp.bfloat16)
    return jnp.concatenate([high, high, low, rest], axis=0)


def column_of(row):
    return jnp.broadcast_to(row, (LANES, LANES)).T


def dot32(a, b):
    return jnp.dot(a, b, preferred_element_type=jnp.float32)


def scan_prepare(
    chunk, docs, step_t, rate, b_t, c_t, packed, start, cum3, tot3, cum_rows, step_rows,
    weight, begin, mix, into,
):
    rows = step_t.shape[1]
    heads = step_t.shape[0]
    n = b_t.shape[0]
    tiles = rows // LANES
    low_lane = lax.broadcasted_iota(jnp.int32, (1, LANES), 1) < LANES // 2
    first = lax.axis_index("ctx") * rows
    position = first + lax.broadcasted_iota(jnp.int32, (8, rows), 1)
    begins = jnp.zeros((8, rows), jnp.int32)
    end = jnp.int32(0)
    for d in range(docs.shape[0]):
        end = end + docs[d]
        begins = jnp.where(position >= end, end, begins)
    begins = begins - first
    start[...] = begins
    begins = begins.astype(jnp.float32)
    rates = -math.log2(math.e) * column_of(
        jnp.concatenate([rate[...], jnp.zeros((1, LANES - heads), jnp.float32)], axis=1)
    )[:heads]
    later = lax.broadcasted_iota(jnp.int32, (LANES, LANES), 1)
    earlier = lax.broadcasted_iota(jnp.int32, (LANES, LANES), 0)
    together = later // chunk == earlier // chunk
    upto = jnp.where(together & (earlier <= later), 1.0, 0.0).astype(jnp.bfloat16)
    after = jnp.where(together & (earlier > later), 1.0, 0.0).astype(jnp.bfloat16)
    ones = jnp.ones((LANES, LANES), jnp.bfloat16)
    everything = jnp.where(earlier <= later, 1.0, 0.0).astype(jnp.bfloat16)
    sums_of = jnp.concatenate([upto, after, everything, ones], axis=1)
    carried = jnp.zeros((heads, LANES), jnp.float32)
    for j in range(tiles):
        at = pl.ds(j * LANES, LANES)
        steps = step_t[:, at].astype(jnp.float32)
        summed = dot32(jnp.concatenate(split3(steps * rates), axis=0), sums_of)
        summed = summed[:heads] + summed[heads : 2 * heads] + summed[2 * heads :]
        cum = summed[:, :LANES]
        suffix = summed[:, LANES : 2 * LANES]
        total = summed[:, 2 * LANES : 3 * LANES] + carried
        carried = carried + summed[:, 3 * LANES :]
        both = jnp.concatenate(split3(cum) + split3(total), axis=0).astype(jnp.float32)
        both = both.T.astype(jnp.bfloat16)
        cum3[at, :] = both[:, : 3 * heads]
        tot3[at, :] = both[:, 3 * heads :]
        for source, kept in ((cum, cum_rows), (steps, step_rows)):
            turned = pltpu.roll(source, LANES // 2, axis=1)
            kept[2 * j] = jnp.where(low_lane, source, pltpu.roll(turned, heads - 1, axis=0))
            kept[2 * j + 1] = jnp.where(
                low_lane, turned, pltpu.roll(source, heads - 1, axis=0)
            )
        starts = column_of(begins[:1, j * LANES : (j + 1) * LANES])
        begin[at, :] = starts
        last = jnp.where(
            low_lane, starts[chunk - 1 : chunk], starts[LANES - 1 : LANES]
        )
        lane_at = (j * LANES + lax.broadcasted_iota(jnp.int32, (1, LANES), 1)).astype(jnp.float32)
        weight[:, at] = jnp.where(lane_at >= last, jnp.exp2(suffix) * steps, 0.0)
        outs = jnp.concatenate([c_t[:, at].astype(jnp.float32)] * (LANES // n), axis=0).T
        row_at = j * LANES + lax.broadcasted_iota(jnp.int32, (LANES, LANES), 0)
        base = (row_at // chunk * chunk).astype(jnp.float32)
        into[0, at, :] = jnp.where(starts < base, outs, 0.0)
        into[1, at, :] = jnp.where(starts < 0.0, outs, 0.0)
        out_n = outs[:, :n].astype(jnp.bfloat16)
        same = dot32(out_n, b_t[:, at])
        lane_in = lax.broadcasted_iota(jnp.int32, (LANES, LANES), 1)
        seen = (lane_in + j * LANES <= row_at) & (
            (lane_in + j * LANES).astype(jnp.float32) >= starts
        )
        same = jnp.where(seen, same, 0.0)
        turned = pltpu.roll(same, LANES // 2, axis=1)
        mix[2 * j] = jnp.where(low_lane, same, turned)[:chunk]
        mix[2 * j + 1] = jnp.where(low_lane, turned, same)[chunk:]
    ending = jnp.where(begins[:1, rows - 1 :] < 0.0, jnp.exp2(carried.T[:1]), 0.0)
    side = jnp.concatenate([ending, jnp.zeros((1, LANES - heads), jnp.float32)], axis=1)
    side = jnp.concatenate(split2(jnp.broadcast_to(side, (n, LANES))), axis=0)
    packed[:, packed.shape[1] - LANES :] = side


def scan_step(
    chunk, step_at, x, skip, b_t, y, lead, packed, cum3, tot3, cum_rows, step_rows, weight,
    begin, mix, into, wide, tail, reaching,
):
    rows = x.shape[0]
    heads = weight.shape[0]
    n = b_t.shape[0]
    chunks = rows // chunk
    block = GROUP * step_at
    spread = widen(3 * heads, heads, block, LANES // 2, GROUP * LANES // 2)
    wide[...] = dot32(cum3[...], spread)
    narrow = widen_pairs(3 * heads, heads, block, n, GROUP // 2 * LANES)
    for pair in range(GROUP // 2):
        part = narrow[:, pair * LANES : (pair + 1) * LANES]
        reaching[pair] = left_parts(jnp.exp2(dot32(cum3[...], part)) * into[0], n)
        lead[step_at, pair] = left_parts(jnp.exp2(dot32(tot3[...], part)) * into[1], n)
    aligned = pl.ds(pl.multiple_of(block, GROUP), GROUP)
    weights = weight[aligned, :]
    for h in range(GROUP):
        high, small = split2(weights[h : h + 1] * b_t[...].astype(jnp.float32))
        row = h // 2 * 4 * n + h % 2 * n
        tail[row : row + n, :] = high
        tail[row + 2 * n : row + 3 * n, :] = small
    skips = jnp.concatenate(
        split3(jnp.concatenate([skip[...]] * 8, axis=0)), axis=1
    )
    skips = dot32(skips, spread)[:1]

    low = lax.broadcasted_iota(jnp.int32, (chunk, LANES), 1) < LANES // 2
    low_n = lax.broadcasted_iota(jnp.int32, (2 * n, LANES), 1) < LANES // 2
    upper_n = lax.broadcasted_iota(jnp.int32, (2 * n, LANES), 0) < n
    own_n = low_n == upper_n
    nothing = jnp.zeros((chunk, LANES), jnp.bfloat16)
    pairs = GROUP // 2
    held = [None] * pairs
    for c in range(chunks):
        at = pl.ds(c * chunk, chunk)
        last = pl.ds(c * chunk + chunk - 1, 1)
        goes_on = begin[last, :] < c * chunk
        cums = cum_rows[c, aligned, :]
        steps = step_rows[c, aligned, :]
        for pair in range(pairs):
            cols = pl.ds(pair * LANES, LANES)
            values = x[at, cols]
            gap = jnp.minimum(wide[at, cols] - cums[2 * pair : 2 * pair + 1], 0.0)
            mixing = jnp.exp2(gap) * mix[c] * steps[2 * pair : 2 * pair + 1]
            left = [mixing.astype(jnp.bfloat16)]
            right = [jnp.where(low, values, nothing), jnp.where(low, nothing, values)]
            if held[pair] is not None:
                right.append(right_parts(jnp.where(own_n, held[pair], 0.0)))
                left.append(reaching[pair, at, :])
            result = dot32(jnp.concatenate(left, axis=1), jnp.concatenate(right, axis=0))
            result = result + skips[:, pair * LANES : (pair + 1) * LANES] * values.astype(jnp.float32)
            y[step_at, at, cols] = result.astype(y.dtype)
            added = dot32(tail[4 * pair * n : 4 * (pair + 1) * n, at], values)
            added = added[: 2 * n] + added[2 * n :]
            if held[pair] is not None:
                kept = jnp.where(goes_on, jnp.exp2(wide[last, cols]), 0.0)
                added = added + kept * held[pair]
            held[pair] = added
    low_16 = lax.broadcasted_iota(jnp.int32, (n, LANES), 1) < LANES // 2
    for pair in range(pairs):
        cols = pl.ds(pl.multiple_of(step_at * pairs * LANES + pair * LANES, LANES), LANES)
        ended = split2(jnp.where(low_16, held[pair][:n], held[pair][n:]))
        packed[:, cols] = jnp.concatenate(ended, axis=0)


def own_prepare(start, values, bias, values_t):
    rows = bias.shape[0]
    key_at = lax.broadcasted_iota(jnp.int32, (rows, rows), 0)
    query_at = lax.broadcasted_iota(jnp.int32, (rows, rows), 1)
    bias[...] = jnp.where((key_at >= start[:1, :]) & (key_at <= query_at), 0.0, NEG)
    for kv in range(values_t.shape[0]):
        values_t[kv] = values[:, kv * HEAD_WIDTH : (kv + 1) * HEAD_WIDTH].T


def own_step(kv, q, keys, values_t, bias, peak, total, acc):
    rows = q.shape[0]
    half = rows // 2
    key_cols = pl.ds(pl.multiple_of(kv * HEAD_WIDTH, HEAD_WIDTH), HEAD_WIDTH)
    for h in range(q.shape[1] // HEAD_WIDTH):
        at = pl.ds(h * HEAD_WIDTH, HEAD_WIDTH)
        for lo in (0, half):
            seen = lo + half
            cols = pl.ds(lo, half)
            top, part, weighted = fold_head(
                HEAD_WIDTH,
                keys[:seen, key_cols],
                values_t[kv, :, :seen],
                q[cols, at],
                bias[:seen, cols],
                None,
            )
            peak[h, :, cols] = top
            total[h, :, cols] = part
            acc[h, :, cols] = (weighted / part).astype(acc.dtype)


def gate_step(gate_at, reach, hops_s, cross_s, y, gate, lead, gated, squares, folded):
    rows = gate.shape[0]
    n = hops_s.shape[1] // 2
    broad = gate.shape[1]
    me = lax.axis_index("ctx")
    odd = lax.rem(me, 2) == 1
    cols_at = pl.ds(pl.multiple_of(gate_at * broad, broad), broad)
    side_at = pl.ds(hops_s.shape[2] - LANES, LANES)
    spread = widen(LANES, LANES, GROUP * gate_at, LANES // 2, broad)
    hops = hops_s.shape[0]

    def from_distance(d, take):
        if d % 2 == 0:
            parts = hops_s[d // 2 - 1, :, take].astype(jnp.float32)
        else:
            j = (d + 1) // 2
            parts = jnp.where(
                odd,
                cross_s[j - 1, :, take].astype(jnp.float32),
                cross_s[j % hops, :, take].astype(jnp.float32),
            )
        return parts[:n] + parts[n:]

    sides = [from_distance(d, side_at)[:8] for d in range(1, reach + 1)]
    high, low = split2(jnp.concatenate(sides, axis=0))
    through = dot32(high, spread) + dot32(low, spread)
    incoming = jnp.zeros((n, broad), jnp.float32)
    for d in range(reach, 0, -1):
        passed = through[8 * (d - 1) : 8 * (d - 1) + 1]
        incoming = jnp.where(me >= d, from_distance(d, cols_at) + passed * incoming, 0.0)
    owner = lax.broadcasted_iota(jnp.int32, (n, broad), 1) // (LANES // 2)
    diagonal = []
    for pair in range(GROUP // 2):
        both = [jnp.where(owner == 2 * pair + h, incoming, 0.0) for h in range(2)]
        both = jnp.concatenate(both, axis=0)[:, pair * LANES : (pair + 1) * LANES]
        diagonal.append(right_parts(both))
    for r in range(0, rows, LANES):
        at = pl.ds(r, LANES)
        total = jnp.where(gate_at > 0, folded[at, :], 0.0)
        for tile in range(broad // LANES):
            cols = pl.ds(tile * LANES, LANES)
            g = gate[at, cols].astype(jnp.float32)
            value = y[gate_at, at, cols].astype(jnp.float32)
            value = value + dot32(lead[gate_at, tile, at, :], diagonal[tile])
            value = value * (g / (1.0 + jnp.exp(-g)))
            gated[at, cols] = value.astype(gated.dtype)
            total = total + value * value
        folded[at, :] = total
        squares[:, at] = jnp.sum(total.T.reshape(LANES // 8, 8, LANES), axis=0)


def chain_kernel(
    chunk, plan, hops, reach, docs, x, step_t, rate, skip, b_t, c_t, q, keys, values, gate,
    keys_h, values_h, gated, squares, peak, total, acc, start, hops_kv, cross_kv,
    packed, hops_s, cross_s, y, lead, cum3, tot3, cum_rows, step_rows, weight, begin, mix, into,
    wide, tail, reaching, bias, values_t, folded, send, recv,
):
    scans, owns, gates = plan
    step_at = pl.program_id(0)
    ctx = lax.axis_size("ctx")
    me = lax.axis_index("ctx")
    ahead, behind = lax.rem(me + 2, ctx), lax.rem(me + ctx - 2, ctx)
    odd = lax.rem(me, 2)
    mate = me + 1 - 2 * odd
    width = keys_h.shape[1]
    mesh_id = pl.DeviceIdType.MESH
    sides = [pl.ds(0, width), pl.ds(width, width)]

    def source(kind, hop):
        if kind == 2:
            return packed if hop == 0 else hops_s.at[hop - 1]
        if hop == 0:
            return (keys_h, values_h)[kind]
        return hops_kv.at[hop - 1, :, sides[kind]]

    def forward(kind, hop):
        return pltpu.make_async_remote_copy(
            src_ref=source(kind, hop - 1),
            dst_ref=source(kind, hop),
            send_sem=send.at[kind, hop - 1],
            recv_sem=recv.at[kind, hop - 1],
            device_id={"ctx": ahead},
            device_id_type=mesh_id,
        )

    def swap(kind, hop):
        slot = hop % hops
        return pltpu.make_async_remote_copy(
            src_ref=source(kind, hop),
            dst_ref=cross_s.at[slot] if kind == 2 else cross_kv.at[slot, :, sides[kind]],
            send_sem=send.at[kind, hops + hop],
            recv_sem=recv.at[kind, hops + hop],
            device_id={"ctx": mate},
            device_id_type=mesh_id,
        )

    def sends(hop):
        return {0: odd == 0, hops: odd == 1}.get(hop)

    def gets(hop):
        return {0: odd == 1, hops: odd == 0}.get(hop)

    def under(condition, act):
        if condition is None:
            act()
        else:
            pl.when(condition)(act)

    def launch(kind, hop):
        if hop < hops:
            forward(kind, hop + 1).start()
        under(sends(hop), lambda: swap(kind, hop).start())

    def relay(kind, hop):
        forward(kind, hop).wait_recv()
        launch(kind, hop)

    def finish(kind):
        for hop in range(1, hops + 1):
            forward(kind, hop).wait_send()
        for hop in range(hops + 1):
            under(sends(hop), lambda hop=hop: swap(kind, hop).wait_send())
            under(gets(hop), lambda hop=hop: swap(kind, hop).wait_recv())

    @pl.when(step_at == 0)
    def _():
        barrier = pltpu.get_barrier_semaphore()
        for peer in (ahead, behind, mate):
            pl.semaphore_signal(barrier, inc=1, device_id={"ctx": peer}, device_id_type=mesh_id)
        pl.semaphore_wait(barrier, 3)
        launch(0, 0)
        launch(1, 0)
        scan_prepare(
            chunk, docs, step_t, rate, b_t, c_t, packed, start, cum3, tot3, cum_rows, step_rows,
            weight, begin, mix, into,
        )

    last = scans + owns + gates - 1
    times = []
    for hop in range(1, hops + 1):
        times.append((2, hop, scans + (owns - 1) * hop // (hops + 1) + 1))
        times.append((0, hop, scans // 2 + (scans + owns) * (hop - 1) // (2 * hops) + 1))
        times.append((1, hop, last - gates - 1 + gates * (hop - 1) // hops))
    for step in range(1, last + 1):
        due = [t for t in times if t[2] == step]
        if step == scans:

            @pl.when(step_at == step)
            def _():
                launch(2, 0)

        for kind, hop, _ in due:

            @pl.when(step_at == step)
            def _(kind=kind, hop=hop):
                relay(kind, hop)

    @pl.when(step_at < scans)
    def _():
        scan_step(
            chunk, step_at, x, skip, b_t, y, lead, packed, cum3, tot3, cum_rows, step_rows,
            weight, begin, mix, into, wide, tail, reaching,
        )

    @pl.when(step_at == scans)
    def _():
        own_prepare(start, values, bias, values_t)

    @pl.when((step_at >= scans) & (step_at < scans + owns))
    def _():
        own_at = step_at - scans
        kv = own_at // (owns // values_t.shape[0])
        own_step(kv, q, keys, values_t, bias, peak, total, acc)

    @pl.when(step_at == scans + owns)
    def _():
        finish(2)

    @pl.when(step_at >= scans + owns)
    def _():
        gate_step(
            step_at - scans - owns, reach, hops_s, cross_s, y, gate, lead, gated, squares, folded
        )

    @pl.when(step_at == last)
    def _():
        finish(0)
        finish(1)


def chain(reach, docs, x, step_t, rate, skip, b_t, c_t, q, keys, values, gate):
    rows, channels = x.shape
    heads = step_t.shape[0]
    scans = heads // GROUP
    broad = channels // scans
    n = b_t.shape[0]
    chunk = LANES // 2
    chunks = rows // chunk
    kv_heads = keys.shape[1] // HEAD_WIDTH
    q_heads = q.shape[1] // HEAD_WIDTH
    owns = q_heads // 2
    hops = (reach + 1) // 2
    whole = lambda shape: pl.BlockSpec(shape, lambda i, d: (0,) * len(shape))
    late = scans + owns

    def own_of(i):
        return jnp.clip(i - scans, 0, owns - 1)

    any_space = pl.BlockSpec(memory_space=pl.ANY)
    slots = (hops, rows, 2 * keys.shape[1])
    wide_n = channels + LANES
    return pl.pallas_call(
        functools.partial(chain_kernel, chunk, (scans, owns, scans), hops, reach),
        out_shape=(
            jax.ShapeDtypeStruct((rows, channels), jnp.bfloat16),
            jax.ShapeDtypeStruct((8, rows), jnp.float32),
            jax.ShapeDtypeStruct((q_heads, 1, rows), jnp.float32),
            jax.ShapeDtypeStruct((q_heads, 1, rows), jnp.float32),
            jax.ShapeDtypeStruct((q_heads, HEAD_WIDTH, rows), jnp.bfloat16),
            jax.ShapeDtypeStruct((8, rows), jnp.int32),
            jax.ShapeDtypeStruct(slots, keys.dtype),
            jax.ShapeDtypeStruct(slots, keys.dtype),
        ),
        grid_spec=pltpu.PrefetchScalarGridSpec(
            num_scalar_prefetch=1,
            grid=(scans + owns + scans,),
            in_specs=[
                pl.BlockSpec((rows, broad), lambda i, d: (0, jnp.minimum(i, scans - 1))),
                whole(step_t.shape),
                whole(rate.shape),
                whole(skip.shape),
                whole(b_t.shape),
                whole(c_t.shape),
                pl.BlockSpec((rows, 2 * HEAD_WIDTH), lambda i, d: (0, own_of(i))),
                whole(keys.shape),
                whole(values.shape),
                pl.BlockSpec((rows, broad), lambda i, d: (0, jnp.maximum(i - late, 0))),
                any_space,
                any_space,
            ],
            out_specs=(
                pl.BlockSpec((rows, broad), lambda i, d: (0, jnp.maximum(i - late, 0))),
                whole((8, rows)),
                pl.BlockSpec((2, 1, rows), lambda i, d: (own_of(i), 0, 0)),
                pl.BlockSpec((2, 1, rows), lambda i, d: (own_of(i), 0, 0)),
                pl.BlockSpec((2, HEAD_WIDTH, rows), lambda i, d: (own_of(i), 0, 0)),
                whole((8, rows)),
                any_space,
                any_space,
            ),
            scratch_shapes=[
                pltpu.VMEM((2 * n, wide_n), jnp.bfloat16),
                pltpu.VMEM((hops, 2 * n, wide_n), jnp.bfloat16),
                pltpu.VMEM((hops, 2 * n, wide_n), jnp.bfloat16),
                pltpu.VMEM((scans, rows, broad), jnp.bfloat16),
                pltpu.VMEM((scans, GROUP // 2, rows, LANES), jnp.bfloat16),
                pltpu.VMEM((rows, 3 * heads), jnp.bfloat16),
                pltpu.VMEM((rows, 3 * heads), jnp.bfloat16),
                pltpu.VMEM((chunks, heads, LANES), jnp.float32),
                pltpu.VMEM((chunks, heads, LANES), jnp.float32),
                pltpu.VMEM((heads, rows), jnp.float32),
                pltpu.VMEM((rows, LANES), jnp.float32),
                pltpu.VMEM((chunks, chunk, LANES), jnp.float32),
                pltpu.VMEM((2, rows, LANES), jnp.float32),
                pltpu.VMEM((rows, broad), jnp.float32),
                pltpu.VMEM((2 * GROUP * n, rows), jnp.bfloat16),
                pltpu.VMEM((GROUP // 2, rows, LANES), jnp.bfloat16),
                pltpu.VMEM((rows, rows), jnp.float32),
                pltpu.VMEM((kv_heads, HEAD_WIDTH, rows), jnp.bfloat16),
                pltpu.VMEM((rows, LANES), jnp.float32),
                pltpu.SemaphoreType.DMA((3, 2 * hops + 1)),
                pltpu.SemaphoreType.DMA((3, 2 * hops + 1)),
            ],
        ),
        compiler_params=pltpu.CompilerParams(collective_id=0, has_side_effects=True),
        cost_estimate=pl.CostEstimate(
            flops=32 * rows * chunk * channels,
            bytes_accessed=8 * x.size,
            transcendentals=2 * x.size,
        ),
        name="chain",
    )(docs, x, step_t, rate, skip, b_t, c_t, q, keys, values, gate, keys, values)


def norm_kernel(count, gated, gain, *refs):
    sums, out = refs[:-1], refs[-1]
    total = sums[0][...]
    for other in sums[1:]:
        total = total + other[...]
    total = jnp.sum(total, axis=0, keepdims=True)
    factor = column_of(lax.rsqrt(total / count + 1e-05))
    for tile in range(gated.shape[1] // LANES):
        cols = pl.ds(tile * LANES, LANES)
        out[:, cols] = (gated[:, cols].astype(jnp.float32) * factor * gain[:, cols]).astype(out.dtype)


def normalize(gated, gain, sums, count):
    rows, channels = gated.shape
    return pl.pallas_call(
        functools.partial(norm_kernel, count),
        out_shape=jax.ShapeDtypeStruct((rows, channels), jnp.bfloat16),
        grid=(rows // LANES,),
        in_specs=[
            pl.BlockSpec((LANES, channels), lambda i: (i, 0)),
            pl.BlockSpec((1, channels), lambda i: (0, 0)),
        ]
        + [pl.BlockSpec((8, LANES), lambda i: (0, i))] * len(sums),
        out_specs=pl.BlockSpec((LANES, channels), lambda i: (i, 0)),
        compiler_params=pltpu.CompilerParams(vmem_limit_bytes=VMEM_LIMIT),
        cost_estimate=pl.CostEstimate(
            flops=4 * gated.size, bytes_accessed=4 * gated.size, transcendentals=rows
        ),
        name="normalize",
    )(gated, gain, *sums)


def layer(
    queries,
    keys,
    values,
    block_plan,
    doc_lengths,
    scan_input,
    gate_input,
    step_size,
    decay_rate,
    state_in,
    state_out,
    skip_gain,
    norm_gain,
):
    ctx, tp = lax.axis_size("ctx"), lax.axis_size("tp")
    me = lax.axis_index("ctx")
    rows = queries.shape[0]
    channels = scan_input.shape[1]
    kv_heads = keys.shape[1] // HEAD_WIDTH
    doc_reach = longest_reach(ctx)
    key_reach = min(doc_reach, SPAN - 1)

    gated, squares, peak, total, acc, start, hops_kv, cross_kv = chain(
        doc_reach,
        doc_lengths,
        scan_input,
        step_size.T,
        decay_rate[None, :],
        skip_gain[None, :],
        state_in.T,
        state_out.T,
        queries,
        keys,
        values,
        gate_input,
    )
    odd = me % 2
    hops = hops_kv.shape[0]
    blocks, distances = [], []
    for j in range(hops):
        blocks += [(hops_kv, j), (cross_kv, j)]
        distances += [2 * j + 2, jnp.where(odd == 1, 2 * j + 1, (2 * j - 1) % (2 * hops))]
    distances = jnp.stack(distances).astype(jnp.int32)
    plan_row = lax.dynamic_index_in_dim(block_plan, me, 0, keepdims=False)
    active = (
        jnp.any(plan_row[None, :] == distances[:, None], axis=1)
        & (distances <= key_reach)
        & (me >= distances)
        & (start[0, 0] < -(distances - 1) * rows)
    ).astype(jnp.int32)
    parts = [squares]
    for by in range(1, tp):
        parts.append(lax.ppermute(squares, "tp", [(i, (i + by) % tp) for i in range(tp)]))
    attn_out = attention(queries, (peak, total, acc), blocks, start[:1], active, distances, kv_heads)
    mamba_out = normalize(gated, norm_gain[None, :], parts, channels * tp)
    return (attn_out, mamba_out)


def solution(mesh):
    in_specs = (
        P("ctx", "tp"),
        P("ctx", "tp"),
        P("ctx", "tp"),
        P(),
        P(),
        P("ctx", "tp"),
        P("ctx", "tp"),
        P("ctx", "tp"),
        P("tp"),
        P("ctx", None),
        P("ctx", None),
        P("tp"),
        P("tp"),
    )
    out_specs = (P("ctx", "tp"), P("ctx", "tp"))
    return jax.shard_map(layer, mesh=mesh, in_specs=in_specs, out_specs=out_specs, check_vma=False)
```
